128 devices in a mesh: band: 2 (over x_hi), chan: 64 (over z, y, x_lo, core).
Axes of the slice: x: 4 (x_hi: 2, x_lo: 2; x = x_hi * 2 + x_lo), y: 4, z: 4, core: 2. Of those that a mesh axis runs over, the one named last changes fastest.
Arguments:
- traces: bfloat16 [10240, 12, 4096], P('chan', 'band'), may hold values from -70 to 70, as said below
- band_start: int32 [2], replicated, may hold values from 0 to 1983
- half_width: int32 [2], replicated, may hold values from 12 to 21
Outputs:
- coherence: float32 [2, 10240, 10240], P('band', 'chan')
The draws below stay inside these ranges and needn't reach their ends.
Inputs may be any that keep to these rules, and one draw needn't show every extreme that they name: `traces`: records hold noise and a few waves that reach each channel with its own delay.
All inputs are finite; a program needn't handle non-finite values.
Results may differ from the reference program's by a relative error of at most 0.0044.
Values may be sent and summed in bfloat16 or wider, within the bound.
No kernel may reach another device: no remote copies, remote signals or barrier semaphores. Data moves between devices by JAX's collectives and lax.ppermute only.
A program may use at most 192 MiB of HBM per device.

```python
import math
import jax
import jax.numpy as jnp
from jax import lax

SAMPLES = 4096
BINS = 64
WINDOWS = 12
CHAN_DEV = 160
CHANNELS = 10240
BANDS = 2
N_CHAN = 64


def draw_traces(key, part):
    subkeys = jax.random.split(key, 5)
    noise_field = jnp.clip(jax.random.normal(subkeys[0], (CHANNELS, WINDOWS, SAMPLES), jnp.float32), -4.0, 4.0)
    wave_rows = jnp.clip(jax.random.normal(subkeys[1], (3, WINDOWS, SAMPLES), jnp.float32), -4.0, 4.0)
    gain_rows = jax.random.uniform(subkeys[3], (CHANNELS, 3), jnp.float32, 0.3, 1.0)
    lag_rows = jax.random.randint(subkeys[4], (CHANNELS, 3), 0, SAMPLES)

    def one_channel(packed):
        gain_row, lag_row = packed
        shared = jnp.zeros((WINDOWS, SAMPLES), jnp.float32)
        for source_id in range(3):
            shared = shared + gain_row[source_id] * jnp.roll(wave_rows[source_id], lag_row[source_id], axis=-1)
        return shared
    shared_field = lax.map(one_channel, (gain_rows, lag_rows))
    return (noise_field + shared_field).astype(jnp.bfloat16)


def setup_inputs(seed: int = 0) -> dict:
    keys = jax.random.split(jax.random.key(seed), 4)
    traces = draw_traces(jax.random.fold_in(keys[3], 71), 0)
    band_start = jax.random.randint(keys[1], (BANDS,), 0, SAMPLES // 2 - BINS).astype(jnp.int32)
    half_width = jax.random.randint(keys[2], (BANDS,), BINS // 5, BINS // 3 + 1).astype(jnp.int32)
    return dict(traces=traces, band_start=band_start, half_width=half_width)


def make_table(band_start):
    sample_ids = jnp.arange(SAMPLES, dtype=jnp.int32)
    freq_ids = band_start[:, None] + jnp.arange(BINS, dtype=jnp.int32)[None, :]
    phases = freq_ids[:, :, None] * sample_ids[None, None, :] % SAMPLES
    angles = phases.astype(jnp.float32) * (2.0 * math.pi / SAMPLES)
    amplitude_scale = 1.0 / math.sqrt(SAMPLES)
    cos_sin = jnp.stack([jnp.cos(angles), -jnp.sin(angles)], axis=1) * amplitude_scale
    band_count = band_start.shape[0]
    return jnp.transpose(cos_sin, (3, 0, 1, 2)).reshape(SAMPLES, band_count * 2 * BINS).astype(jnp.bfloat16)

def smoother(half_width):
    row_ids = jnp.arange(BINS, dtype=jnp.int32)[:, None]
    col_ids = jnp.arange(BINS, dtype=jnp.int32)[None, :]
    inside = (jnp.abs(row_ids - col_ids)[None, :, :] <= half_width[:, None, None]).astype(jnp.float32)
    return inside / lax.optimization_barrier(jnp.sum(inside, axis=1, keepdims=True))

def whiten(trace_block, dft_table, smooth):
    rows_here = trace_block.shape[0]
    wins_here = trace_block.shape[1]
    band_count = smooth.shape[0]
    flat = trace_block.reshape(rows_here * wins_here, SAMPLES)
    spectra = jnp.dot(flat, dft_table, preferred_element_type=jnp.float32)
    spectra = spectra.reshape(rows_here, wins_here, band_count, 2, BINS)
    amplitude = jnp.sqrt(spectra[:, :, :, 0] * spectra[:, :, :, 0] + spectra[:, :, :, 1] * spectra[:, :, :, 1])
    smoothed = jnp.einsum('cwbj,bjk->cwbk', amplitude, smooth, precision=lax.Precision.HIGHEST)
    whitened = spectra / (smoothed[:, :, :, None, :] + 1e-05)
    return whitened.reshape(rows_here, wins_here, band_count, 2 * BINS).astype(jnp.bfloat16)

def normalize(band_rows):
    values = band_rows.astype(jnp.float32)
    energy = lax.optimization_barrier(jnp.sum(values * values, axis=(1, 2)))
    normed = values / jnp.sqrt(energy + 1e-06)[:, None, None]
    return normed.reshape(band_rows.shape[0], band_rows.shape[1] * band_rows.shape[2]).astype(jnp.bfloat16)

def reference(traces, band_start, half_width):
    dft_table = make_table(band_start)
    smooth = smoother(half_width)
    blocks = traces.reshape(N_CHAN, CHAN_DEV, WINDOWS, SAMPLES)

    def one_block(trace_block):
        return whiten(trace_block, dft_table, smooth)
    whitened = lax.map(one_block, blocks).reshape(CHANNELS, WINDOWS, BANDS, 2 * BINS)
    per_band = []
    for band_id in range(BANDS):
        normed = normalize(whitened[:, :, band_id, :])
        per_band.append(jnp.dot(normed, normed.T, preferred_element_type=jnp.float32))
    return jnp.stack(per_band)
```

```python
import math

import jax
import jax.numpy as jnp
from jax import lax
from jax.experimental import pallas as pl
from jax.experimental.pallas import tpu as pltpu
from jax.sharding import PartitionSpec as P

SAMPLES = 4096
BINS = 64
WINS = 6
ROWS = 160
DEPTH = 1536
GROUP = 640
STEP_ROWS = 320
PARTS = 128
TURN = 2.0 * math.pi / SAMPLES


def whiten_kernel(meta, x_ref, keep_ref, send_ref, table, mask, share):
    @pl.when(pl.program_id(0) == 0)
    def _():
        lane = lax.broadcasted_iota(jnp.int32, (1, 128), 1)
        freq = jnp.where(lane < BINS, meta[0] + lane, meta[1] + lane - BINS)
        coarse = lax.broadcasted_iota(jnp.int32, (SAMPLES // PARTS, 128), 0) * PARTS
        fine = lax.broadcasted_iota(jnp.int32, (PARTS, 128), 0)
        angle_a = ((freq * coarse) & (SAMPLES - 1)).astype(jnp.float32) * TURN
        angle_b = ((freq * fine) & (SAMPLES - 1)).astype(jnp.float32) * TURN
        root = 1.0 / math.sqrt(SAMPLES)
        cos_a, sin_a = jnp.cos(angle_a) * root, jnp.sin(angle_a) * root
        cos_b, sin_b = jnp.cos(angle_b), jnp.sin(angle_b)
        for part in range(SAMPLES // PARTS):
            rows = pl.ds(part * PARTS, PARTS)
            ca, sa = cos_a[part : part + 1], sin_a[part : part + 1]
            table[rows, 0:128] = (ca * cos_b - sa * sin_b).astype(jnp.bfloat16)
            table[rows, 128:256] = (-(sa * cos_b + ca * sin_b)).astype(jnp.bfloat16)
        row = lax.broadcasted_iota(jnp.int32, (256, 128), 0) & 127
        col = lax.broadcasted_iota(jnp.int32, (256, 128), 1)
        half = jnp.where(col < BINS, meta[2], meta[3])
        inside = ((row < BINS) == (col < BINS)) & (jnp.abs(row - col) <= half)
        mask[...] = inside.astype(jnp.float32).astype(jnp.bfloat16)
        bin_id = lane & (BINS - 1)
        width = jnp.where(lane < BINS, meta[2], meta[3])
        count = jnp.minimum(bin_id + width, BINS - 1) - jnp.maximum(bin_id - width, 0) + 1
        share[...] = 1.0 / count.astype(jnp.float32)

    spectra = jnp.dot(x_ref[...], table[...], preferred_element_type=jnp.float32)
    re, im = spectra[:, :128], spectra[:, 128:]
    amplitude = jnp.sqrt(re * re + im * im)
    high = amplitude.astype(jnp.bfloat16)
    low = (amplitude - high.astype(jnp.float32)).astype(jnp.bfloat16)
    sums = jnp.dot(
        jnp.concatenate([high, low], axis=1), mask[...], preferred_element_type=jnp.float32
    )
    gain = 1.0 / (sums * share[...] + 1e-05)
    re, im = re * gain, im * gain
    turned = pltpu.roll(im, BINS, 1)
    first = lax.broadcasted_iota(jnp.int32, re.shape, 1) < BINS
    band0 = jnp.where(first, re, turned)
    band1 = jnp.where(first, turned, re)
    mine = meta[4] == 0
    keep_ref[...] = jnp.where(mine, band0, band1).astype(jnp.bfloat16)
    send_ref[...] = jnp.where(mine, band1, band0).astype(jnp.bfloat16)


def whiten(flat, meta):
    total = flat.shape[0]
    out = jax.ShapeDtypeStruct((total, 128), jnp.bfloat16)
    block = pl.BlockSpec((STEP_ROWS, 128), lambda i, m: (i, 0))
    return pl.pallas_call(
        whiten_kernel,
        grid_spec=pltpu.PrefetchScalarGridSpec(
            num_scalar_prefetch=1,
            grid=(total // STEP_ROWS,),
            in_specs=[pl.BlockSpec((STEP_ROWS, SAMPLES), lambda i, m: (i, 0))],
            out_specs=[block, block],
            scratch_shapes=[
                pltpu.VMEM((SAMPLES, 256), jnp.bfloat16),
                pltpu.VMEM((256, 128), jnp.bfloat16),
                pltpu.VMEM((1, 128), jnp.float32),
            ],
        ),
        out_shape=[out, out],
        compiler_params=pltpu.CompilerParams(vmem_limit_bytes=40 << 20),
        name="whiten",
    )(meta, flat)


def normalize_kernel(keep_ref, got_ref, out_ref):
    energy = jnp.zeros((ROWS, 128), jnp.float32)
    for ref in (keep_ref, got_ref):
        for win in range(WINS):
            value = ref[win * ROWS : (win + 1) * ROWS, :].astype(jnp.float32)
            energy = energy + value * value
    scale = 1.0 / jnp.sqrt(jnp.sum(energy, axis=1, keepdims=True) + 1e-06)
    for side, ref in enumerate((keep_ref, got_ref)):
        for win in range(WINS):
            value = ref[win * ROWS : (win + 1) * ROWS, :].astype(jnp.float32)
            at = (side * WINS + win) * 128
            out_ref[:, at : at + 128] = (value * scale).astype(jnp.bfloat16)


def normalize(keep, got):
    return pl.pallas_call(
        normalize_kernel,
        out_shape=jax.ShapeDtypeStruct((ROWS, DEPTH), jnp.bfloat16),
        name="normalize",
    )(keep, got)


def cross_kernel(swap, meta, *refs):
    row_refs, col_refs = refs[:4], refs[4:8]
    mine_ref, c_ref, x_ref, xc_ref = refs[8:12]
    rows, cols, row_sems, col_sems = refs[12:]
    for i in range(4):
        pltpu.make_async_copy(
            row_refs[i], rows.at[pl.ds(i * ROWS, ROWS)], row_sems.at[i]
        ).start()

    def fetch(order):
        for i in range(4):
            pltpu.make_async_copy(
                col_refs[order[i]], cols.at[pl.ds(i * ROWS, ROWS)], col_sems.at[i]
            ).start()

    @pl.when(meta[0] == 0)
    def _():
        fetch((0, 1, 2, 3))

    @pl.when(meta[0] != 0)
    def _():
        fetch(swap)

    for i in range(4):
        pltpu.make_async_copy(
            row_refs[i], rows.at[pl.ds(i * ROWS, ROWS)], row_sems.at[i]
        ).wait()
        pltpu.make_async_copy(
            col_refs[i], cols.at[pl.ds(i * ROWS, ROWS)], col_sems.at[i]
        ).wait()
    product = lax.dot_general(
        rows[...], cols[...], (((1,), (1,)), ((), ())), preferred_element_type=jnp.float32
    )
    mine_ref[...] = product[:ROWS]
    c_ref[...] = product[ROWS : 2 * ROWS].astype(jnp.bfloat16)
    x_ref[...] = product[2 * ROWS : 3 * ROWS].astype(jnp.bfloat16)
    xc_ref[...] = product[3 * ROWS :].astype(jnp.bfloat16)


def cross(place, rows, cols, swap):
    narrow = jax.ShapeDtypeStruct((ROWS, GROUP), jnp.bfloat16)
    return pl.pallas_call(
        lambda *refs: cross_kernel(swap, *refs),
        in_specs=[pl.BlockSpec(memory_space=pltpu.SMEM)] + [pl.BlockSpec(memory_space=pl.ANY)] * 8,
        out_shape=[jax.ShapeDtypeStruct((ROWS, GROUP), jnp.float32), narrow, narrow, narrow],
        scratch_shapes=[
            pltpu.VMEM((4 * ROWS, DEPTH), jnp.bfloat16),
            pltpu.VMEM((4 * ROWS, DEPTH), jnp.bfloat16),
            pltpu.SemaphoreType.DMA((4,)),
            pltpu.SemaphoreType.DMA((4,)),
        ],
        compiler_params=pltpu.CompilerParams(vmem_limit_bytes=32 << 20),
        name="cross",
    )(place, *rows, *cols)


def place_kernel(meta, own, got_c, got_x, got_xc, *refs):
    out, buf, sems = refs[-3:]
    for slot in range(4):

        @pl.when(meta[0] == slot)
        def _():
            for g in range(4):
                for flip, piece in enumerate((own, got_c, got_x, got_xc)):
                    at = (slot ^ flip) * ROWS
                    value = piece[:, g * ROWS : (g + 1) * ROWS].astype(jnp.float32)
                    buf[g, :, at : at + ROWS] = value

    copies = []
    for g in range(4):
        start = pl.multiple_of(meta[1 + g] * GROUP, 128)
        copies.append(
            pltpu.make_async_copy(buf.at[g], out.at[:, pl.ds(start, GROUP)], sems.at[g])
        )
        copies[-1].start()
    for copy in copies:
        copy.wait()


def place_group(meta, pieces, out):
    vmem = pl.BlockSpec(memory_space=pltpu.VMEM)
    prior = () if out is None else (out,)
    return pl.pallas_call(
        place_kernel,
        in_specs=[pl.BlockSpec(memory_space=pltpu.SMEM)]
        + [vmem] * 4
        + [pl.BlockSpec(memory_space=pl.ANY)] * len(prior),
        out_specs=pl.BlockSpec(memory_space=pl.ANY),
        out_shape=jax.ShapeDtypeStruct((ROWS, 16 * GROUP), jnp.float32),
        scratch_shapes=[
            pltpu.VMEM((4, ROWS, GROUP), jnp.float32),
            pltpu.SemaphoreType.DMA((4,)),
        ],
        input_output_aliases={5: 0} if prior else {},
        compiler_params=pltpu.CompilerParams(vmem_limit_bytes=32 << 20),
        name="place",
    )(meta, *pieces, *prior)


def unit(index):
    return index // 16, index // 4 % 4, index // 2 % 2, index % 2


def join(z, y, x, c):
    return (z % 4) * 16 + (y % 4) * 4 + x * 2 + c


def from_first(shift):
    pairs = []
    for dst in range(64):
        z, y, x, c = unit(dst)
        src = join(z + shift, y, x, c) if c == 0 else join(z, y + shift, x, c)
        pairs.append((src, dst))
    return pairs


def from_second(shift):
    pairs = []
    for dst in range(64):
        z, y, x, c = unit(dst)
        src = join(z, y + shift, x, c) if c == 0 else join(z + shift, y, x, c)
        pairs.append((src, dst))
    return pairs


def flip(bits):
    return [(i, i ^ bits) for i in range(64)]


GROUPS = (
    (((1, 0), (0, 1), (-1, 0), (0, -1)), (1, 0, 3, 2)),
    (((1, 1), (-1, -1), (1, -1), (-1, 1)), (0, 1, 3, 2)),
    (((0, 0), (2, 2), (2, 0), (0, 2)), (0, 1, 3, 2)),
    (((1, 2), (2, 1), (-1, 2), (2, -1)), (1, 0, 3, 2)),
)


def local(traces, band_start, half_width):
    band = lax.axis_index("band").astype(jnp.int32)
    chan = lax.axis_index("chan").astype(jnp.int32)
    meta = jnp.concatenate([band_start, half_width, band[None]])
    flat = jnp.transpose(traces, (1, 0, 2)).reshape(WINS * ROWS, SAMPLES)
    keep, send = whiten(flat, meta)
    got = lax.ppermute(send, "band", [(0, 1), (1, 0)])
    own = normalize(keep, got)

    def move(value, pairs):
        return lax.ppermute(value, "chan", pairs)

    near = {}
    near[0, 0] = own
    near[1, 0] = move(own, from_first(1))
    near[-1, 0] = move(own, from_first(-1))
    row_x = move(own, flip(2))
    row_c = move(own, flip(1))
    near[0, 1] = move(own, from_second(1))
    near[0, -1] = move(own, from_second(-1))
    row_xc = move(row_x, flip(1))
    near[2, 0] = move(near[1, 0], from_first(1))
    for du in (1, -1, 2):
        for dv in (1, -1):
            near[du, dv] = move(near[du, 0], from_second(dv))
    for du, dv in ((0, 1), (1, 1), (-1, -1), (2, -1)):
        near[du, 2] = move(near[du, dv], from_second(dv))

    z, y, _, c = unit(chan)
    place = c[None]
    rows = (own, row_c, row_x, row_xc)
    out = None
    for offsets, swap in GROUPS:
        mine, to_c, to_x, to_xc = cross(place, rows, [near[o] for o in offsets], swap)
        pieces = (mine, move(to_c, flip(1)), move(to_x, flip(2)), move(to_xc, flip(3)))
        where = [((z + dz) & 3) * 4 + ((y + dy) & 3) for dz, dy in offsets]
        out = place_group(jnp.stack([chan & 3] + where), pieces, out)
    return out[None]


def solution(mesh):
    placed = (P("chan", "band", None), P(), P())
    return jax.shard_map(
        local, mesh=mesh, in_specs=placed, out_specs=P("band", "chan", None), check_vma=False
    )
```

```python
import math

import jax
import jax.numpy as jnp
from jax import lax
from jax.experimental import pallas as pl
from jax.experimental.pallas import tpu as pltpu
from jax.sharding import PartitionSpec as P

SAMPLES = 4096
BINS = 64
WINS = 6
ROWS = 160
DEPTH = 1536
GROUP = 640
STEP_ROWS = 320
CHUNK = 1024
LOAD = 2
PARTS = 128
TURN = 2.0 * math.pi / SAMPLES


def whiten_kernel(start, width_ref, x_hbm, keep_ref, send_ref, held, table, total, sems):
    def fetch(piece):
        block = pl.ds(piece * ROWS, ROWS)
        return pltpu.make_async_copy(x_hbm.at[block], held.at[block], sems.at[piece])

    for piece in range(0, WINS):
        fetch(piece).start()
    lane = lax.broadcasted_iota(jnp.int32, (1, 128), 1)
    freq = jnp.where(lane < BINS, start[0] + lane, start[1] + lane - BINS)
    coarse = lax.broadcasted_iota(jnp.int32, (SAMPLES // PARTS, 128), 0) * PARTS
    fine = lax.broadcasted_iota(jnp.int32, (PARTS, 128), 0)
    angle_a = ((freq * coarse) & (SAMPLES - 1)).astype(jnp.float32) * TURN
    angle_b = ((freq * fine) & (SAMPLES - 1)).astype(jnp.float32) * TURN
    root = 1.0 / math.sqrt(SAMPLES)
    cos_a, sin_a = jnp.cos(angle_a) * root, jnp.sin(angle_a) * root
    cos_b, sin_b = jnp.cos(angle_b), jnp.sin(angle_b)
    row = lax.broadcasted_iota(jnp.int32, (256, 128), 0) & 127
    col = lax.broadcasted_iota(jnp.int32, (256, 128), 1)
    half = jnp.where(col < BINS, width_ref[0], width_ref[1])
    inside = ((row < BINS) == (col < BINS)) & (jnp.abs(row - col) <= half)
    mask = inside.astype(jnp.float32).astype(jnp.bfloat16)
    bin_id = lane & (BINS - 1)
    width = jnp.where(lane < BINS, width_ref[0], width_ref[1])
    count = jnp.minimum(bin_id + width, BINS - 1) - jnp.maximum(bin_id - width, 0) + 1
    share = 1.0 / count.astype(jnp.float32)
    first = lax.broadcasted_iota(jnp.int32, (STEP_ROWS, 128), 1) < BINS
    mine = lax.axis_index("band") == 0

    for part in range(SAMPLES // PARTS):
        at = slice(part * PARTS, (part + 1) * PARTS)
        ca, sa = cos_a[part : part + 1], sin_a[part : part + 1]
        table[at, 0:128] = (ca * cos_b - sa * sin_b).astype(jnp.bfloat16)
        table[at, 128:256] = (-(sa * cos_b + ca * sin_b)).astype(jnp.bfloat16)

    for piece in range(0, WINS, LOAD):
        for i in range(LOAD):
            fetch(piece + i).wait()
        block = slice(piece * ROWS, (piece + LOAD) * ROWS)
        for at in range(0, SAMPLES, CHUNK):
            product = jnp.dot(
                held[block, at : at + CHUNK],
                table[at : at + CHUNK, :],
                preferred_element_type=jnp.float32,
            )
            if at == 0:
                total[block, :] = product
            else:
                total[block, :] += product

    for at in range(0, WINS * ROWS, STEP_ROWS):
        block = slice(at, at + STEP_ROWS)
        re, im = total[block, :128], total[block, 128:]
        amplitude = jnp.sqrt(re * re + im * im)
        high = amplitude.astype(jnp.bfloat16)
        low = (amplitude - high.astype(jnp.float32)).astype(jnp.bfloat16)
        sums = jnp.dot(
            jnp.concatenate([high, low], axis=1), mask, preferred_element_type=jnp.float32
        )
        gain = 1.0 / (sums * share + 1e-05)
        re, im = re * gain, im * gain
        turned = pltpu.roll(im, BINS, 1)
        band0 = jnp.where(first, re, turned)
        band1 = jnp.where(first, turned, re)
        keep_ref[block, :] = jnp.where(mine, band0, band1).astype(jnp.bfloat16)
        send_ref[block, :] = jnp.where(mine, band1, band0).astype(jnp.bfloat16)


def whiten(flat, band_start, half_width):
    total = flat.shape[0]
    out = jax.ShapeDtypeStruct((total, 128), jnp.bfloat16)
    return pl.pallas_call(
        whiten_kernel,
        in_specs=[
            pl.BlockSpec(memory_space=pltpu.SMEM),
            pl.BlockSpec(memory_space=pltpu.SMEM),
            pl.BlockSpec(memory_space=pltpu.HBM),
        ],
        out_shape=[out, out],
        scratch_shapes=[
            pltpu.VMEM((total, SAMPLES), jnp.bfloat16),
            pltpu.VMEM((SAMPLES, 256), jnp.bfloat16),
            pltpu.VMEM((total, 256), jnp.float32),
            pltpu.SemaphoreType.DMA((WINS,)),
        ],
        compiler_params=pltpu.CompilerParams(vmem_limit_bytes=57 << 20),
        name="whiten",
    )(band_start, half_width, flat)


def normalize_kernel(keep_ref, got_ref, out_ref):
    energy = jnp.zeros((ROWS, 128), jnp.float32)
    for ref in (keep_ref, got_ref):
        for win in range(WINS):
            value = ref[win * ROWS : (win + 1) * ROWS, :].astype(jnp.float32)
            energy = energy + value * value
    scale = 1.0 / jnp.sqrt(jnp.sum(energy, axis=1, keepdims=True) + 1e-06)
    for side, ref in enumerate((keep_ref, got_ref)):
        for win in range(WINS):
            value = ref[win * ROWS : (win + 1) * ROWS, :].astype(jnp.float32)
            at = (side * WINS + win) * 128
            out_ref[:, at : at + 128] = (value * scale).astype(jnp.bfloat16)


def normalize(keep, got):
    return pl.pallas_call(
        normalize_kernel,
        out_shape=jax.ShapeDtypeStruct((ROWS, DEPTH), jnp.bfloat16),
        compiler_params=pltpu.CompilerParams(vmem_limit_bytes=8 << 20),
        name="normalize",
    )(keep, got)


def stack_kernel(*refs):
    at = 0
    for ref in refs[:-1]:
        refs[-1][at : at + ref.shape[0], :] = ref[...]
        at += ref.shape[0]


def stack(*shards):
    total = sum(shard.shape[0] for shard in shards)
    return pl.pallas_call(
        stack_kernel,
        out_shape=jax.ShapeDtypeStruct((total, DEPTH), jnp.bfloat16),
        compiler_params=pltpu.CompilerParams(vmem_limit_bytes=8 << 20),
        name="stack",
    )(*shards)


def cross_kernel(rows, first, second, mine_ref, c_ref, x_ref, *refs):
    cols = refs[-1]
    half = GROUP // 2
    cols[:half, :] = first[...]
    cols[half:, :] = second[...]
    product = lax.dot_general(
        rows[...], cols[...], (((1,), (1,)), ((), ())), preferred_element_type=jnp.float32
    )
    mine_ref[...] = product[:ROWS]
    to_x = product[ROWS : 2 * ROWS].astype(jnp.bfloat16)
    c_ref[...] = product[2 * ROWS : 3 * ROWS].astype(jnp.bfloat16)
    to_xc = product[3 * ROWS :].astype(jnp.bfloat16)
    if len(refs) == 1:
        x_ref[:, :GROUP] = to_x
        x_ref[:, GROUP:] = to_xc
    else:
        x_ref[...] = to_x
        refs[0][...] = to_xc


def cross(rows, first, second, merged):
    narrow = jax.ShapeDtypeStruct((ROWS, GROUP), jnp.bfloat16)
    wide = jax.ShapeDtypeStruct((ROWS, 2 * GROUP), jnp.bfloat16)
    mine = jax.ShapeDtypeStruct((ROWS, GROUP), jnp.float32)
    return pl.pallas_call(
        cross_kernel,
        out_shape=[mine, narrow, wide] if merged else [mine, narrow, narrow, narrow],
        scratch_shapes=[pltpu.VMEM((4 * ROWS, DEPTH), jnp.bfloat16)],
        compiler_params=pltpu.CompilerParams(vmem_limit_bytes=12 << 20),
        cost_estimate=pl.CostEstimate(
            flops=2 * GROUP * GROUP * DEPTH, transcendentals=0, bytes_accessed=12 << 20
        ),
        name="cross",
    )(rows, first, second)


NEAR = (0, 1, -1, 2)
GROUPS = (
    ((0, 0), (1, 0), (-1, 0), (2, 0)),
    ((0, 1), (1, 1), (-1, -1), (2, -1)),
    ((-1, 1), (2, 1), (0, -1), (1, -1)),
    ((0, 2), (1, 2), (-1, 2), (2, 2)),
)
SPOT = {offset: (g, i) for g, group in enumerate(GROUPS) for i, offset in enumerate(group)}


def place_kernel(blocks, groups, kinds, *refs):
    out, buf, sems = refs[-3:]
    pieces = {}
    for index, kind in enumerate(kinds):
        pieces[kind] = refs[index]
    chan = lax.axis_index("chan")
    z, y, spot, core = chan // 16, (chan // 4) % 4, chan % 4, chan % 2

    def copy(n):
        du, dv = blocks[n]
        dz, dy = jnp.where(core == 0, du, dv), jnp.where(core == 0, dv, du)
        unit_id = ((z + dz + 4) % 4) * 4 + (y + dy + 4) % 4
        start = pl.multiple_of(unit_id * GROUP, 128)
        return pltpu.make_async_copy(buf.at[n], out.at[:, pl.ds(start, GROUP)], sems.at[n])

    for slot in range(4):

        @pl.when(spot == slot)
        def _():
            for n, (du, dv) in enumerate(blocks):
                for turn in range(4):
                    g, i = SPOT[(dv, du) if turn % 2 else (du, dv)]
                    ref, base = pieces[turn, g], 0
                    if ref.shape[1] == 2 * GROUP and turn == 3:
                        base = GROUP
                    value = ref[:, base + i * ROWS : base + (i + 1) * ROWS].astype(jnp.float32)
                    at = (slot ^ turn) * ROWS
                    buf[n, :, at : at + ROWS] = value
                copy(n).start()

    for n in range(len(blocks)):
        copy(n).wait()


def place(blocks, pieces, out):
    vmem = pl.BlockSpec(memory_space=pltpu.VMEM)
    groups = sorted({g for _, g in pieces})
    kinds = sorted(pieces)
    prior = () if out is None else (out,)
    return pl.pallas_call(
        lambda *refs: place_kernel(blocks, groups, kinds, *refs),
        in_specs=[vmem] * len(kinds) + [pl.BlockSpec(memory_space=pl.ANY)] * len(prior),
        out_specs=pl.BlockSpec(memory_space=pl.ANY),
        out_shape=jax.ShapeDtypeStruct((ROWS, 16 * GROUP), jnp.float32),
        scratch_shapes=[
            pltpu.VMEM((len(blocks), ROWS, GROUP), jnp.float32),
            pltpu.SemaphoreType.DMA((len(blocks),)),
        ],
        input_output_aliases={len(kinds): 0} if prior else {},
        compiler_params=pltpu.CompilerParams(vmem_limit_bytes=16 << 20),
        name="place",
    )(*[pieces[kind] for kind in kinds], *prior)


def unit(index):
    return index // 16, index // 4 % 4, index // 2 % 2, index % 2


def join(z, y, x, c):
    return (z % 4) * 16 + (y % 4) * 4 + x * 2 + c


def from_first(shift):
    pairs = []
    for dst in range(64):
        z, y, x, c = unit(dst)
        src = join(z + shift, y, x, c) if c == 0 else join(z, y + shift, x, c)
        pairs.append((src, dst))
    return pairs


def from_second(shift):
    pairs = []
    for dst in range(64):
        z, y, x, c = unit(dst)
        src = join(z, y + shift, x, c) if c == 0 else join(z + shift, y, x, c)
        pairs.append((src, dst))
    return pairs


def flip(bits):
    return [(i, i ^ bits) for i in range(64)]


def local(traces, band_start, half_width):
    flat = jnp.transpose(traces, (1, 0, 2)).reshape(WINS * ROWS, SAMPLES)
    keep, send = whiten(flat, band_start, half_width)
    got = lax.ppermute(send, "band", [(0, 1), (1, 0)])
    own = normalize(keep, got)
    hold = lax.optimization_barrier

    def move(value, pairs):
        return lax.ppermute(value, "chan", pairs)

    ahead, behind = move(own, from_first(1)), move(own, from_first(-1))
    far, over = move(own, from_first(2)), move(own, flip(2))
    ahead, behind, far = hold((ahead, behind, far))
    pair0, pair1 = stack(own, ahead), stack(behind, far)
    up0, down1 = move(pair0, from_second(1)), move(pair1, from_second(-1))
    up1, down0 = move(pair1, from_second(1)), move(pair0, from_second(-1))
    mates = stack(own, over)
    rows = stack(mates, move(mates, flip(1)))
    mine0, c0, x0 = cross(rows, pair0, pair1, True)
    x0 = move(x0, flip(2))
    c0 = move(c0, flip(1))
    mine1, c1, x1 = cross(rows, up0, down1, True)
    x1 = move(x1, flip(2))
    up0, down1, up1, down0, x0, c0, x1, c1 = hold((up0, down1, up1, down0, x0, c0, x1, c1))
    up2, down2 = move(up0, from_second(1)), move(down1, from_second(-1))
    mine2, c2, x2 = cross(rows, up1, down0, True)
    x2 = move(x2, flip(2))
    xc0 = move(x0, flip(1))
    c1 = move(c1, flip(1))
    c2 = move(c2, flip(1))
    up2, down2, x2, c2, xc0, c1, x1 = hold((up2, down2, x2, c2, xc0, c1, x1))
    mine3, c3, x3, xc3 = cross(rows, up2, down2, False)
    x3, xc3, c3 = move(x3, flip(2)), move(xc3, flip(3)), move(c3, flip(1))
    xc1 = move(x1, flip(1))
    xc2 = move(x2, flip(1))
    early = [(du, dv) for du in NEAR for dv in NEAR if du != 2 and dv != 2]
    late = [(du, dv) for du in NEAR for dv in NEAR if du == 2 or dv == 2]
    pieces = {}
    for g, parts in enumerate(((mine0, c0, x0, xc0), (mine1, c1, x1, xc1), (mine2, c2, x2, xc2))):
        for turn in range(4):
            pieces[turn, g] = parts[turn]
    out = place(early, pieces, None)
    for turn, part in enumerate((mine3, c3, x3, xc3)):
        pieces[turn, 3] = part
    return place(late, pieces, out)[None]


def solution(mesh):
    placed = (P("chan", "band", None), P(), P())
    return jax.shard_map(
        local, mesh=mesh, in_specs=placed, out_specs=P("band", "chan", None), check_vma=False
    )
```

```python
import math

import jax
import jax.numpy as jnp
from jax import lax
from jax.experimental import pallas as pl
from jax.experimental.pallas import tpu as pltpu
from jax.sharding import PartitionSpec as P

SAMPLES = 4096
BINS = 64
WINS = 6
ROWS = 160
DEPTH = 1536
GROUP = 640
STEP_ROWS = 320
CHUNK = 1024
LOAD = 2
PARTS = 128
TURN = 2.0 * math.pi / SAMPLES


def whiten_kernel(start, width_ref, x_hbm, keep_ref, send_ref, held, table, total, sems):
    def fetch(piece):
        block = pl.ds(piece * ROWS, ROWS)
        return pltpu.make_async_copy(x_hbm.at[block], held.at[block], sems.at[piece])

    for piece in range(0, WINS):
        fetch(piece).start()
    lane = lax.broadcasted_iota(jnp.int32, (1, 128), 1)
    freq = jnp.where(lane < BINS, start[0] + lane, start[1] + lane - BINS)
    coarse = lax.broadcasted_iota(jnp.int32, (SAMPLES // PARTS, 128), 0) * PARTS
    fine = lax.broadcasted_iota(jnp.int32, (PARTS, 128), 0)
    angle_a = ((freq * coarse) & (SAMPLES - 1)).astype(jnp.float32) * TURN
    angle_b = ((freq * fine) & (SAMPLES - 1)).astype(jnp.float32) * TURN
    root = 1.0 / math.sqrt(SAMPLES)
    cos_a, sin_a = jnp.cos(angle_a) * root, jnp.sin(angle_a) * root
    cos_b, sin_b = jnp.cos(angle_b), jnp.sin(angle_b)
    row = lax.broadcasted_iota(jnp.int32, (256, 128), 0) & 127
    col = lax.broadcasted_iota(jnp.int32, (256, 128), 1)
    half = jnp.where(col < BINS, width_ref[0], width_ref[1])
    inside = ((row < BINS) == (col < BINS)) & (jnp.abs(row - col) <= half)
    mask = inside.astype(jnp.float32).astype(jnp.bfloat16)
    bin_id = lane & (BINS - 1)
    width = jnp.where(lane < BINS, width_ref[0], width_ref[1])
    count = jnp.minimum(bin_id + width, BINS - 1) - jnp.maximum(bin_id - width, 0) + 1
    share = 1.0 / count.astype(jnp.float32)
    first = lax.broadcasted_iota(jnp.int32, (STEP_ROWS, 128), 1) < BINS
    mine = lax.axis_index("band") == 0

    for part in range(SAMPLES // PARTS):
        at = slice(part * PARTS, (part + 1) * PARTS)
        ca, sa = cos_a[part : part + 1], sin_a[part : part + 1]
        table[at, 0:128] = (ca * cos_b - sa * sin_b).astype(jnp.bfloat16)
        table[at, 128:256] = (-(sa * cos_b + ca * sin_b)).astype(jnp.bfloat16)

    for piece in range(0, WINS, LOAD):
        for i in range(LOAD):
            fetch(piece + i).wait()
        block = slice(piece * ROWS, (piece + LOAD) * ROWS)
        for at in range(0, SAMPLES, CHUNK):
            product = jnp.dot(
                held[block, at : at + CHUNK],
                table[at : at + CHUNK, :],
                preferred_element_type=jnp.float32,
            )
            if at == 0:
                total[block, :] = product
            else:
                total[block, :] += product

    for at in range(0, WINS * ROWS, STEP_ROWS):
        block = slice(at, at + STEP_ROWS)
        re, im = total[block, :128], total[block, 128:]
        amplitude = jnp.sqrt(re * re + im * im)
        high = amplitude.astype(jnp.bfloat16)
        low = (amplitude - high.astype(jnp.float32)).astype(jnp.bfloat16)
        sums = jnp.dot(
            jnp.concatenate([high, low], axis=1), mask, preferred_element_type=jnp.float32
        )
        gain = 1.0 / (sums * share + 1e-05)
        re, im = re * gain, im * gain
        turned = pltpu.roll(im, BINS, 1)
        band0 = jnp.where(first, re, turned)
        band1 = jnp.where(first, turned, re)
        keep_ref[block, :] = jnp.where(mine, band0, band1).astype(jnp.bfloat16)
        send_ref[block, :] = jnp.where(mine, band1, band0).astype(jnp.bfloat16)


def whiten(flat, band_start, half_width):
    total = flat.shape[0]
    out = jax.ShapeDtypeStruct((total, 128), jnp.bfloat16)
    return pl.pallas_call(
        whiten_kernel,
        in_specs=[
            pl.BlockSpec(memory_space=pltpu.SMEM),
            pl.BlockSpec(memory_space=pltpu.SMEM),
            pl.BlockSpec(memory_space=pltpu.HBM),
        ],
        out_shape=[out, out],
        scratch_shapes=[
            pltpu.VMEM((total, SAMPLES), jnp.bfloat16),
            pltpu.VMEM((SAMPLES, 256), jnp.bfloat16),
            pltpu.VMEM((total, 256), jnp.float32),
            pltpu.SemaphoreType.DMA((WINS,)),
        ],
        compiler_params=pltpu.CompilerParams(vmem_limit_bytes=53 << 20),
        name="whiten",
    )(band_start, half_width, flat)


def normalize_kernel(keep_ref, got_ref, out_ref):
    energy = jnp.zeros((ROWS, 128), jnp.float32)
    for ref in (keep_ref, got_ref):
        for win in range(WINS):
            value = ref[win * ROWS : (win + 1) * ROWS, :].astype(jnp.float32)
            energy = energy + value * value
    scale = 1.0 / jnp.sqrt(jnp.sum(energy, axis=1, keepdims=True) + 1e-06)
    for side, ref in enumerate((keep_ref, got_ref)):
        for win in range(WINS):
            value = ref[win * ROWS : (win + 1) * ROWS, :].astype(jnp.float32)
            at = (side * WINS + win) * 128
            out_ref[:, at : at + 128] = (value * scale).astype(jnp.bfloat16)


def normalize(keep, got):
    return pl.pallas_call(
        normalize_kernel,
        out_shape=jax.ShapeDtypeStruct((ROWS, DEPTH), jnp.bfloat16),
        compiler_params=pltpu.CompilerParams(vmem_limit_bytes=8 << 20),
        name="normalize",
    )(keep, got)


def stack_kernel(*refs):
    at = 0
    for ref in refs[:-1]:
        refs[-1][at : at + ref.shape[0], :] = ref[...]
        at += ref.shape[0]


def stack(*shards):
    total = sum(shard.shape[0] for shard in shards)
    return pl.pallas_call(
        stack_kernel,
        out_shape=jax.ShapeDtypeStruct((total, DEPTH), jnp.bfloat16),
        compiler_params=pltpu.CompilerParams(vmem_limit_bytes=8 << 20),
        name="stack",
    )(*shards)


def cross_kernel(rows, first, second, mine_ref, c_ref, x_ref, *refs):
    cols = refs[-1]
    half = GROUP // 2
    cols[:half, :] = first[...]
    cols[half:, :] = second[...]
    product = lax.dot_general(
        rows[...], cols[...], (((1,), (1,)), ((), ())), preferred_element_type=jnp.float32
    )
    mine_ref[...] = product[:ROWS]
    to_x = product[ROWS : 2 * ROWS].astype(jnp.bfloat16)
    c_ref[...] = product[2 * ROWS : 3 * ROWS].astype(jnp.bfloat16)
    to_xc = product[3 * ROWS :].astype(jnp.bfloat16)
    if len(refs) == 1:
        x_ref[:, :GROUP] = to_x
        x_ref[:, GROUP:] = to_xc
    else:
        x_ref[...] = to_x
        refs[0][...] = to_xc


def cross(rows, first, second, merged):
    narrow = jax.ShapeDtypeStruct((ROWS, GROUP), jnp.bfloat16)
    wide = jax.ShapeDtypeStruct((ROWS, 2 * GROUP), jnp.bfloat16)
    mine = jax.ShapeDtypeStruct((ROWS, GROUP), jnp.float32)
    return pl.pallas_call(
        cross_kernel,
        out_shape=[mine, narrow, wide] if merged else [mine, narrow, narrow, narrow],
        scratch_shapes=[pltpu.VMEM((4 * ROWS, DEPTH), jnp.bfloat16)],
        compiler_params=pltpu.CompilerParams(vmem_limit_bytes=12 << 20),
        cost_estimate=pl.CostEstimate(
            flops=2 * GROUP * GROUP * DEPTH, transcendentals=0, bytes_accessed=12 << 20
        ),
        name="cross",
    )(rows, first, second)


NEAR = (0, 1, -1, 2)
GROUPS = (
    ((0, 0), (1, 0), (-1, 0), (2, 0)),
    ((0, 1), (1, 1), (-1, -1), (2, -1)),
    ((-1, 1), (2, 1), (0, -1), (1, -1)),
    ((0, 2), (1, 2), (-1, 2), (2, 2)),
)
SPOT = {offset: (g, i) for g, group in enumerate(GROUPS) for i, offset in enumerate(group)}


def place_kernel(blocks, groups, kinds, *refs):
    out, buf, sems = refs[-3:]
    pieces = {}
    for index, kind in enumerate(kinds):
        pieces[kind] = refs[index]
    chan = lax.axis_index("chan")
    z, y, spot, core = chan // 16, (chan // 4) % 4, chan % 4, chan % 2

    def copy(n):
        du, dv = blocks[n]
        dz, dy = jnp.where(core == 0, du, dv), jnp.where(core == 0, dv, du)
        unit_id = ((z + dz + 4) % 4) * 4 + (y + dy + 4) % 4
        start = pl.multiple_of(unit_id * GROUP, 128)
        return pltpu.make_async_copy(buf.at[n], out.at[:, pl.ds(start, GROUP)], sems.at[n])

    for slot in range(4):

        @pl.when(spot == slot)
        def _():
            for n, (du, dv) in enumerate(blocks):
                for turn in range(4):
                    g, i = SPOT[(dv, du) if turn % 2 else (du, dv)]
                    ref, base = pieces[turn, g], 0
                    if ref.shape[1] == 2 * GROUP and turn == 3:
                        base = GROUP
                    value = ref[:, base + i * ROWS : base + (i + 1) * ROWS].astype(jnp.float32)
                    at = (slot ^ turn) * ROWS
                    buf[n, :, at : at + ROWS] = value
                copy(n).start()

    for n in range(len(blocks)):
        copy(n).wait()


def place(blocks, pieces, out):
    vmem = pl.BlockSpec(memory_space=pltpu.VMEM)
    groups = sorted({g for _, g in pieces})
    kinds = sorted(pieces)
    prior = () if out is None else (out,)
    return pl.pallas_call(
        lambda *refs: place_kernel(blocks, groups, kinds, *refs),
        in_specs=[vmem] * len(kinds) + [pl.BlockSpec(memory_space=pl.ANY)] * len(prior),
        out_specs=pl.BlockSpec(memory_space=pl.ANY),
        out_shape=jax.ShapeDtypeStruct((ROWS, 16 * GROUP), jnp.float32),
        scratch_shapes=[
            pltpu.VMEM((len(blocks), ROWS, GROUP), jnp.float32),
            pltpu.SemaphoreType.DMA((len(blocks),)),
        ],
        input_output_aliases={len(kinds): 0} if prior else {},
        compiler_params=pltpu.CompilerParams(vmem_limit_bytes=16 << 20),
        name="place",
    )(*[pieces[kind] for kind in kinds], *prior)


def unit(index):
    return index // 16, index // 4 % 4, index // 2 % 2, index % 2


def join(z, y, x, c):
    return (z % 4) * 16 + (y % 4) * 4 + x * 2 + c


def from_first(shift):
    pairs = []
    for dst in range(64):
        z, y, x, c = unit(dst)
        src = join(z + shift, y, x, c) if c == 0 else join(z, y + shift, x, c)
        pairs.append((src, dst))
    return pairs


def from_second(shift):
    pairs = []
    for dst in range(64):
        z, y, x, c = unit(dst)
        src = join(z, y + shift, x, c) if c == 0 else join(z + shift, y, x, c)
        pairs.append((src, dst))
    return pairs


def flip(bits):
    return [(i, i ^ bits) for i in range(64)]


def local(traces, band_start, half_width):
    flat = jnp.transpose(traces, (1, 0, 2)).reshape(WINS * ROWS, SAMPLES)
    keep, send = whiten(flat, band_start, half_width)
    got = lax.ppermute(send, "band", [(0, 1), (1, 0)])
    own = normalize(keep, got)
    hold = lax.optimization_barrier

    def move(value, pairs):
        return lax.ppermute(value, "chan", pairs)

    ahead, behind = move(own, from_first(1)), move(own, from_first(-1))
    far, over = move(own, from_first(2)), move(own, flip(2))
    ahead, behind, far, over = hold((ahead, behind, far, over))
    mates = stack(own, over)
    across = move(mates, flip(1))
    pair0, pair1 = stack(own, ahead), stack(behind, far)
    up0, down1 = move(pair0, from_second(1)), move(pair1, from_second(-1))
    up1, down0 = move(pair1, from_second(1)), move(pair0, from_second(-1))
    rows = stack(mates, across)
    mine0, c0, x0 = cross(rows, pair0, pair1, True)
    x0 = move(x0, flip(2))
    c0 = move(c0, flip(1))
    mine1, c1, x1 = cross(rows, up0, down1, True)
    x1, x0, c0, up0, down1 = hold((x1, x0, c0, up0, down1))
    x1 = move(x1, flip(2))
    up2, down2 = move(up0, from_second(1)), move(down1, from_second(-1))
    xc0 = move(x0, flip(1))
    c1 = move(c1, flip(1))
    mine2, c2, x2 = cross(rows, up1, down0, True)
    x2, x1, c1, xc0 = hold((x2, x1, c1, xc0))
    x2 = move(x2, flip(2))
    xc1 = move(x1, flip(1))
    c2 = move(c2, flip(1))
    mine3, c3, x3, xc3 = cross(rows, up2, down2, False)
    x3, xc3, x2, c2, xc1 = hold((x3, xc3, x2, c2, xc1))
    x3, xc3, c3 = move(x3, flip(2)), move(xc3, flip(3)), move(c3, flip(1))
    xc2 = move(x2, flip(1))
    early = [(du, dv) for du in NEAR for dv in NEAR if du != 2 and dv != 2]
    late = [(du, dv) for du in NEAR for dv in NEAR if du == 2 or dv == 2]
    pieces = {}
    for g, parts in enumerate(((mine0, c0, x0, xc0), (mine1, c1, x1, xc1), (mine2, c2, x2, xc2))):
        for turn in range(4):
            pieces[turn, g] = parts[turn]
    out = place(early, pieces, None)
    for turn, part in enumerate((mine3, c3, x3, xc3)):
        pieces[turn, 3] = part
    return place(late, pieces, out)[None]


def solution(mesh):
    placed = (P("chan", "band", None), P(), P())
    return jax.shard_map(
        local, mesh=mesh, in_specs=placed, out_specs=P("band", "chan", None), check_vma=False
    )
```

```python
import math

import jax
import jax.numpy as jnp
from jax import lax
from jax.experimental import pallas as pl
from jax.experimental.pallas import tpu as pltpu
from jax.sharding import PartitionSpec as P

SAMPLES = 4096
BINS = 64
WINS = 6
ROWS = 160
DEPTH = 1536
GROUP = 640
STEP_ROWS = 320
CHUNK = 1024
LOAD = 2
PARTS = 128
TURN = 2.0 * math.pi / SAMPLES


def whiten_kernel(bands, x_hbm, keep_ref, send_ref, held, table, total, sems):
    def fetch(piece):
        block = pl.ds(piece * ROWS, ROWS)
        return pltpu.make_async_copy(x_hbm.at[block], held.at[block], sems.at[piece])

    for piece in range(0, WINS):
        fetch(piece).start()
    lane = lax.broadcasted_iota(jnp.int32, (1, 128), 1)
    freq = jnp.where(lane < BINS, bands[0] + lane, bands[1] + lane - BINS)
    coarse = lax.broadcasted_iota(jnp.int32, (SAMPLES // PARTS, 128), 0) * PARTS
    fine = lax.broadcasted_iota(jnp.int32, (PARTS, 128), 0)
    angle_a = ((freq * coarse) & (SAMPLES - 1)).astype(jnp.float32) * TURN
    angle_b = ((freq * fine) & (SAMPLES - 1)).astype(jnp.float32) * TURN
    root = 1.0 / math.sqrt(SAMPLES)
    cos_a, sin_a = jnp.cos(angle_a) * root, jnp.sin(angle_a) * root
    cos_b, sin_b = jnp.cos(angle_b), jnp.sin(angle_b)
    row = lax.broadcasted_iota(jnp.int32, (256, 128), 0) & 127
    col = lax.broadcasted_iota(jnp.int32, (256, 128), 1)
    half = jnp.where(col < BINS, bands[2], bands[3])
    inside = ((row < BINS) == (col < BINS)) & (jnp.abs(row - col) <= half)
    mask = inside.astype(jnp.float32).astype(jnp.bfloat16)
    bin_id = lane & (BINS - 1)
    width = jnp.where(lane < BINS, bands[2], bands[3])
    count = jnp.minimum(bin_id + width, BINS - 1) - jnp.maximum(bin_id - width, 0) + 1
    share = 1.0 / count.astype(jnp.float32)
    first = lax.broadcasted_iota(jnp.int32, (STEP_ROWS, 128), 1) < BINS
    mine = lax.axis_index("band") == 0

    for part in range(SAMPLES // PARTS):
        at = slice(part * PARTS, (part + 1) * PARTS)
        ca, sa = cos_a[part : part + 1], sin_a[part : part + 1]
        table[at, 0:128] = (ca * cos_b - sa * sin_b).astype(jnp.bfloat16)
        table[at, 128:256] = (-(sa * cos_b + ca * sin_b)).astype(jnp.bfloat16)

    for piece in range(0, WINS, LOAD):
        for i in range(LOAD):
            fetch(piece + i).wait()
        block = slice(piece * ROWS, (piece + LOAD) * ROWS)
        for at in range(0, SAMPLES, CHUNK):
            product = jnp.dot(
                held[block, at : at + CHUNK],
                table[at : at + CHUNK, :],
                preferred_element_type=jnp.float32,
            )
            if at == 0:
                total[block, :] = product
            else:
                total[block, :] += product

    for at in range(0, WINS * ROWS, STEP_ROWS):
        block = slice(at, at + STEP_ROWS)
        re, im = total[block, :128], total[block, 128:]
        amplitude = jnp.sqrt(re * re + im * im)
        high = amplitude.astype(jnp.bfloat16)
        low = (amplitude - high.astype(jnp.float32)).astype(jnp.bfloat16)
        sums = jnp.dot(
            jnp.concatenate([high, low], axis=1), mask, preferred_element_type=jnp.float32
        )
        gain = 1.0 / (sums * share + 1e-05)
        re, im = re * gain, im * gain
        turned = pltpu.roll(im, BINS, 1)
        band0 = jnp.where(first, re, turned)
        band1 = jnp.where(first, turned, re)
        keep_ref[block, :] = jnp.where(mine, band0, band1).astype(jnp.bfloat16)
        send_ref[block, :] = jnp.where(mine, band1, band0).astype(jnp.bfloat16)


def whiten(flat, bands):
    total = flat.shape[0]
    out = jax.ShapeDtypeStruct((total, 128), jnp.bfloat16)
    return pl.pallas_call(
        whiten_kernel,
        in_specs=[
            pl.BlockSpec(memory_space=pltpu.SMEM),
            pl.BlockSpec(memory_space=pltpu.HBM),
        ],
        out_shape=[out, out],
        scratch_shapes=[
            pltpu.VMEM((total, SAMPLES), jnp.bfloat16),
            pltpu.VMEM((SAMPLES, 256), jnp.bfloat16),
            pltpu.VMEM((total, 256), jnp.float32),
            pltpu.SemaphoreType.DMA((WINS,)),
        ],
        compiler_params=pltpu.CompilerParams(vmem_limit_bytes=53 << 20),
        name="whiten",
    )(bands, flat)


def normalize_kernel(keep_ref, got_ref, out_ref):
    energy = jnp.zeros((ROWS, 128), jnp.float32)
    for ref in (keep_ref, got_ref):
        for win in range(WINS):
            value = ref[win * ROWS : (win + 1) * ROWS, :].astype(jnp.float32)
            energy = energy + value * value
    scale = 1.0 / jnp.sqrt(jnp.sum(energy, axis=1, keepdims=True) + 1e-06)
    for side, ref in enumerate((keep_ref, got_ref)):
        for win in range(WINS):
            value = ref[win * ROWS : (win + 1) * ROWS, :].astype(jnp.float32)
            at = (side * WINS + win) * 128
            out_ref[:, at : at + 128] = (value * scale).astype(jnp.bfloat16)


def normalize(keep, got):
    return pl.pallas_call(
        normalize_kernel,
        out_shape=jax.ShapeDtypeStruct((ROWS, DEPTH), jnp.bfloat16),
        compiler_params=pltpu.CompilerParams(vmem_limit_bytes=8 << 20),
        name="normalize",
    )(keep, got)


def stack_kernel(*refs):
    at = 0
    for ref in refs[:-1]:
        refs[-1][at : at + ref.shape[0], :] = ref[...]
        at += ref.shape[0]


def stack(*shards):
    total = sum(shard.shape[0] for shard in shards)
    return pl.pallas_call(
        stack_kernel,
        out_shape=jax.ShapeDtypeStruct((total, DEPTH), jnp.bfloat16),
        compiler_params=pltpu.CompilerParams(vmem_limit_bytes=8 << 20),
        name="stack",
    )(*shards)


def cross_kernel(rows, first, second, mine_ref, c_ref, x_ref, *refs):
    cols = refs[-1]
    half = GROUP // 2
    cols[:half, :] = first[...]
    cols[half:, :] = second[...]
    product = lax.dot_general(
        rows[...], cols[...], (((1,), (1,)), ((), ())), preferred_element_type=jnp.float32
    )
    mine_ref[...] = product[:ROWS]
    to_x = product[ROWS : 2 * ROWS].astype(jnp.bfloat16)
    c_ref[...] = product[2 * ROWS : 3 * ROWS].astype(jnp.bfloat16)
    to_xc = product[3 * ROWS :].astype(jnp.bfloat16)
    if len(refs) == 1:
        x_ref[:, :GROUP] = to_x
        x_ref[:, GROUP:] = to_xc
    else:
        x_ref[...] = to_x
        refs[0][...] = to_xc


def cross(rows, first, second, merged):
    narrow = jax.ShapeDtypeStruct((ROWS, GROUP), jnp.bfloat16)
    wide = jax.ShapeDtypeStruct((ROWS, 2 * GROUP), jnp.bfloat16)
    mine = jax.ShapeDtypeStruct((ROWS, GROUP), jnp.float32)
    return pl.pallas_call(
        cross_kernel,
        out_shape=[mine, narrow, wide] if merged else [mine, narrow, narrow, narrow],
        scratch_shapes=[pltpu.VMEM((4 * ROWS, DEPTH), jnp.bfloat16)],
        compiler_params=pltpu.CompilerParams(vmem_limit_bytes=12 << 20),
        cost_estimate=pl.CostEstimate(
            flops=2 * GROUP * GROUP * DEPTH, transcendentals=0, bytes_accessed=12 << 20
        ),
        name="cross",
    )(rows, first, second)


FIRST = 512


def first_cross_kernel(rows, pair0, pair1, mine_ref, c_ref, x_ref, here_ref, cols):
    cols[:ROWS, :] = pair0[ROWS:, :]
    cols[ROWS : 3 * ROWS, :] = pair1[...]
    cols[3 * ROWS :, :] = pair0[:ROWS, :]
    product = lax.dot_general(
        rows[...], cols[...], (((1,), (1,)), ((), ())), preferred_element_type=jnp.float32
    )
    mine_ref[...] = product[:ROWS]
    x_ref[:, :FIRST] = product[ROWS : 2 * ROWS, :FIRST].astype(jnp.bfloat16)
    c_ref[...] = product[2 * ROWS : 3 * ROWS].astype(jnp.bfloat16)
    x_ref[:, FIRST:] = product[3 * ROWS :, :FIRST].astype(jnp.bfloat16)
    here_ref[...] = lax.dot_general(
        rows[:ROWS, :], rows[...], (((1,), (1,)), ((), ())), preferred_element_type=jnp.float32
    )


def first_cross(rows, pair0, pair1):
    wide = jax.ShapeDtypeStruct((ROWS, GROUP), jnp.float32)
    return pl.pallas_call(
        first_cross_kernel,
        out_shape=[
            wide,
            jax.ShapeDtypeStruct((ROWS, GROUP), jnp.bfloat16),
            jax.ShapeDtypeStruct((ROWS, 2 * FIRST), jnp.bfloat16),
            wide,
        ],
        scratch_shapes=[pltpu.VMEM((4 * ROWS, DEPTH), jnp.bfloat16)],
        compiler_params=pltpu.CompilerParams(vmem_limit_bytes=12 << 20),
        cost_estimate=pl.CostEstimate(
            flops=2 * GROUP * GROUP * DEPTH, transcendentals=0, bytes_accessed=12 << 20
        ),
        name="cross",
    )(rows, pair0, pair1)


NEAR = (0, 1, -1, 2)
GROUPS = (
    ((1, 0), (-1, 0), (2, 0), (0, 0)),
    ((0, 1), (1, 1), (-1, -1), (2, -1)),
    ((-1, 1), (2, 1), (0, -1), (1, -1)),
    ((0, 2), (1, 2), (-1, 2), (2, 2)),
)
SPOT = {offset: (g, i) for g, group in enumerate(GROUPS) for i, offset in enumerate(group)}


def place_kernel(blocks, kinds, *refs):
    out, buf, sems = refs[-3:]
    pieces = {}
    for index, kind in enumerate(kinds):
        pieces[kind] = refs[index]
    chan = lax.axis_index("chan")
    z, y, spot, core = chan // 16, (chan // 4) % 4, chan % 4, chan % 2

    def copy(n):
        du, dv = blocks[n]
        dz, dy = jnp.where(core == 0, du, dv), jnp.where(core == 0, dv, du)
        unit_id = ((z + dz + 4) % 4) * 4 + (y + dy + 4) % 4
        start = pl.multiple_of(unit_id * GROUP, 128)
        return pltpu.make_async_copy(buf.at[n], out.at[:, pl.ds(start, GROUP)], sems.at[n])

    for slot in range(4):

        @pl.when(spot == slot)
        def _():
            for n, (du, dv) in enumerate(blocks):
                for turn in range(4):
                    g, i = SPOT[(dv, du) if turn % 2 else (du, dv)]
                    if (du, dv) == (0, 0):
                        ref, base, i = pieces[4, 0], 0, (0, 2, 1, 3)[turn]
                    else:
                        ref = pieces[turn, g]
                        split = turn == 3 and ref.shape[1] > GROUP
                        base = ref.shape[1] // 2 if split else 0
                    value = ref[:, base + i * ROWS : base + (i + 1) * ROWS].astype(jnp.float32)
                    at = (slot ^ turn) * ROWS
                    buf[n, :, at : at + ROWS] = value
                copy(n).start()

    for n in range(len(blocks)):
        copy(n).wait()


def place(blocks, pieces, out):
    vmem = pl.BlockSpec(memory_space=pltpu.VMEM)
    used = {(4, 0)} if (0, 0) in blocks else set()
    for du, dv in blocks:
        if (du, dv) != (0, 0):
            for turn in range(4):
                used.add((turn, SPOT[(dv, du) if turn % 2 else (du, dv)][0]))
    kinds = sorted(used, key=lambda kind: (kind[1], kind[0]))
    prior = () if out is None else (out,)
    return pl.pallas_call(
        lambda *refs: place_kernel(blocks, kinds, *refs),
        in_specs=[vmem] * len(kinds) + [pl.BlockSpec(memory_space=pl.ANY)] * len(prior),
        out_specs=pl.BlockSpec(memory_space=pl.ANY),
        out_shape=jax.ShapeDtypeStruct((ROWS, 16 * GROUP), jnp.float32),
        scratch_shapes=[
            pltpu.VMEM((len(blocks), ROWS, GROUP), jnp.float32),
            pltpu.SemaphoreType.DMA((len(blocks),)),
        ],
        input_output_aliases={len(kinds): 0} if prior else {},
        compiler_params=pltpu.CompilerParams(vmem_limit_bytes=16 << 20),
        name="place",
    )(*[pieces[kind] for kind in kinds], *prior)


def unit(index):
    return index // 16, index // 4 % 4, index // 2 % 2, index % 2


def join(z, y, x, c):
    return (z % 4) * 16 + (y % 4) * 4 + x * 2 + c


def from_first(shift):
    pairs = []
    for dst in range(64):
        z, y, x, c = unit(dst)
        src = join(z + shift, y, x, c) if c == 0 else join(z, y + shift, x, c)
        pairs.append((src, dst))
    return pairs


def from_second(shift):
    pairs = []
    for dst in range(64):
        z, y, x, c = unit(dst)
        src = join(z, y + shift, x, c) if c == 0 else join(z + shift, y, x, c)
        pairs.append((src, dst))
    return pairs


def flip(bits):
    return [(i, i ^ bits) for i in range(64)]


def local(traces, band_start, half_width):
    flat = jnp.transpose(traces, (1, 0, 2)).reshape(WINS * ROWS, SAMPLES)
    keep, send = whiten(flat, jnp.concatenate([band_start, half_width]))
    got = lax.ppermute(send, "band", [(0, 1), (1, 0)])
    own = normalize(keep, got)
    hold = lax.optimization_barrier

    def move(value, pairs):
        return lax.ppermute(value, "chan", pairs)

    over, far = move(own, flip(2)), move(own, from_first(2))
    behind, ahead = move(own, from_first(-1)), move(own, from_first(1))
    over, far, behind, ahead = hold((over, far, behind, ahead))
    mates = stack(own, over)
    across = move(mates, flip(1))
    pair0, pair1 = stack(own, ahead), stack(behind, far)
    up0, down1 = move(pair0, from_second(1)), move(pair1, from_second(-1))
    up1, down0 = move(pair1, from_second(1)), move(pair0, from_second(-1))
    rows = stack(mates, across)
    mine0, c0, x0, here = first_cross(rows, pair0, pair1)
    x0 = move(x0, flip(2))
    c0 = move(c0, flip(1))
    mine1, c1, x1 = cross(rows, up0, down1, True)
    x1, x0, c0, up0, down1 = hold((x1, x0, c0, up0, down1))
    up2, down2 = move(up0, from_second(1)), move(down1, from_second(-1))
    x1 = move(x1, flip(2))
    xc0 = move(x0, flip(1))
    c1 = move(c1, flip(1))
    mine2, c2, x2 = cross(rows, up1, down0, True)
    x2, c1, xc0 = hold((x2, c1, xc0))
    x2 = move(x2, flip(2))
    xc1 = move(x1, flip(1))
    c2 = move(c2, flip(1))
    mine3, c3, x3, xc3 = cross(rows, up2, down2, False)
    x3, xc3, x2, c2, xc1 = hold((x3, xc3, x2, c2, xc1))
    x3, xc3, c3 = move(x3, flip(2)), move(xc3, flip(3)), move(c3, flip(1))
    xc2 = move(x2, flip(1))
    early = [(du, dv) for du in NEAR for dv in NEAR if du != 2 and dv != 2]
    middle = [(0, 2), (1, 2), (-1, 2)]
    late = [(2, dv) for dv in NEAR]
    pieces = {(4, 0): here}
    for g, parts in enumerate(((mine0, c0, x0, xc0), (mine1, c1, x1, xc1), (mine2, c2, x2, xc2))):
        for turn in range(4):
            pieces[turn, g] = parts[turn]
    out = place(early, pieces, None)
    pieces[0, 3], pieces[2, 3] = mine3, x3
    out = place(middle, pieces, out)
    pieces[1, 3], pieces[3, 3] = c3, xc3
    return place(late, pieces, out)[None]


def solution(mesh):
    placed = (P("chan", "band", None), P(), P())
    return jax.shard_map(
        local, mesh=mesh, in_specs=placed, out_specs=P("band", "chan", None), check_vma=False
    )
```

```python
import math

import jax
import jax.numpy as jnp
from jax import lax
from jax.experimental import pallas as pl
from jax.experimental.pallas import tpu as pltpu
from jax.sharding import PartitionSpec as P

SAMPLES = 4096
BINS = 64
WINS = 6
ROWS = 160
DEPTH = 1536
GROUP = 640
STEP_ROWS = 320
CHUNK = 1024
LOAD = 2
PARTS = 128
TURN = 2.0 * math.pi / SAMPLES


def whiten_kernel(bands, x_hbm, keep_ref, send_ref, held, table, total, sems):
    def fetch(piece):
        block = pl.ds(piece * ROWS, ROWS)
        return pltpu.make_async_copy(x_hbm.at[block], held.at[block], sems.at[piece])

    for piece in range(0, WINS):
        fetch(piece).start()
    lane = lax.broadcasted_iota(jnp.int32, (1, 128), 1)
    freq = jnp.where(lane < BINS, bands[0] + lane, bands[1] + lane - BINS)
    coarse = lax.broadcasted_iota(jnp.int32, (SAMPLES // PARTS, 128), 0) * PARTS
    fine = lax.broadcasted_iota(jnp.int32, (PARTS, 128), 0)
    angle_a = ((freq * coarse) & (SAMPLES - 1)).astype(jnp.float32) * TURN
    angle_b = ((freq * fine) & (SAMPLES - 1)).astype(jnp.float32) * TURN
    root = 1.0 / math.sqrt(SAMPLES)
    cos_a, sin_a = jnp.cos(angle_a) * root, jnp.sin(angle_a) * root
    cos_b, sin_b = jnp.cos(angle_b), jnp.sin(angle_b)
    row = lax.broadcasted_iota(jnp.int32, (256, 128), 0) & 127
    col = lax.broadcasted_iota(jnp.int32, (256, 128), 1)
    half = jnp.where(col < BINS, bands[2], bands[3])
    inside = ((row < BINS) == (col < BINS)) & (jnp.abs(row - col) <= half)
    mask = inside.astype(jnp.float32).astype(jnp.bfloat16)
    bin_id = lane & (BINS - 1)
    width = jnp.where(lane < BINS, bands[2], bands[3])
    count = jnp.minimum(bin_id + width, BINS - 1) - jnp.maximum(bin_id - width, 0) + 1
    share = 1.0 / count.astype(jnp.float32)
    first = lax.broadcasted_iota(jnp.int32, (STEP_ROWS, 128), 1) < BINS
    mine = lax.axis_index("band") == 0

    for part in range(SAMPLES // PARTS):
        at = slice(part * PARTS, (part + 1) * PARTS)
        ca, sa = cos_a[part : part + 1], sin_a[part : part + 1]
        table[at, 0:128] = (ca * cos_b - sa * sin_b).astype(jnp.bfloat16)
        table[at, 128:256] = (-(sa * cos_b + ca * sin_b)).astype(jnp.bfloat16)

    for piece in range(0, WINS, LOAD):
        for i in range(LOAD):
            fetch(piece + i).wait()
        block = slice(piece * ROWS, (piece + LOAD) * ROWS)
        for at in range(0, SAMPLES, CHUNK):
            product = jnp.dot(
                held[block, at : at + CHUNK],
                table[at : at + CHUNK, :],
                preferred_element_type=jnp.float32,
            )
            if at == 0:
                total[block, :] = product
            else:
                total[block, :] += product

    for at in range(0, WINS * ROWS, STEP_ROWS):
        block = slice(at, at + STEP_ROWS)
        re, im = total[block, :128], total[block, 128:]
        amplitude = jnp.sqrt(re * re + im * im)
        high = amplitude.astype(jnp.bfloat16)
        low = (amplitude - high.astype(jnp.float32)).astype(jnp.bfloat16)
        sums = jnp.dot(
            jnp.concatenate([high, low], axis=1), mask, preferred_element_type=jnp.float32
        )
        gain = 1.0 / (sums * share + 1e-05)
        re, im = re * gain, im * gain
        turned = pltpu.roll(im, BINS, 1)
        band0 = jnp.where(first, re, turned)
        band1 = jnp.where(first, turned, re)
        keep_ref[block, :] = jnp.where(mine, band0, band1).astype(jnp.bfloat16)
        send_ref[block, :] = jnp.where(mine, band1, band0).astype(jnp.bfloat16)


def whiten(flat, bands):
    total = flat.shape[0]
    out = jax.ShapeDtypeStruct((total, 128), jnp.bfloat16)
    return pl.pallas_call(
        whiten_kernel,
        in_specs=[
            pl.BlockSpec(memory_space=pltpu.SMEM),
            pl.BlockSpec(memory_space=pltpu.HBM),
        ],
        out_shape=[out, out],
        scratch_shapes=[
            pltpu.VMEM((total, SAMPLES), jnp.bfloat16),
            pltpu.VMEM((SAMPLES, 256), jnp.bfloat16),
            pltpu.VMEM((total, 256), jnp.float32),
            pltpu.SemaphoreType.DMA((WINS,)),
        ],
        compiler_params=pltpu.CompilerParams(vmem_limit_bytes=53 << 20),
        name="whiten",
    )(bands, flat)


def normalize_kernel(keep_ref, got_ref, out_ref):
    energy = jnp.zeros((ROWS, 128), jnp.float32)
    for ref in (keep_ref, got_ref):
        for win in range(WINS):
            value = ref[win * ROWS : (win + 1) * ROWS, :].astype(jnp.float32)
            energy = energy + value * value
    scale = 1.0 / jnp.sqrt(jnp.sum(energy, axis=1, keepdims=True) + 1e-06)
    for side, ref in enumerate((keep_ref, got_ref)):
        for win in range(WINS):
            value = ref[win * ROWS : (win + 1) * ROWS, :].astype(jnp.float32)
            at = (side * WINS + win) * 128
            out_ref[:, at : at + 128] = (value * scale).astype(jnp.bfloat16)


def normalize(keep, got):
    return pl.pallas_call(
        normalize_kernel,
        out_shape=jax.ShapeDtypeStruct((ROWS, DEPTH), jnp.bfloat16),
        compiler_params=pltpu.CompilerParams(vmem_limit_bytes=8 << 20),
        name="normalize",
    )(keep, got)


def stack_kernel(*refs):
    at = 0
    for ref in refs[:-1]:
        refs[-1][at : at + ref.shape[0], :] = ref[...]
        at += ref.shape[0]


def stack(*shards):
    total = sum(shard.shape[0] for shard in shards)
    return pl.pallas_call(
        stack_kernel,
        out_shape=jax.ShapeDtypeStruct((total, DEPTH), jnp.bfloat16),
        compiler_params=pltpu.CompilerParams(vmem_limit_bytes=8 << 20),
        name="stack",
    )(*shards)


def cross_kernel(rows, first, second, mine_ref, c_ref, x_ref, *refs):
    cols = refs[-1]
    half = GROUP // 2
    cols[:half, :] = first[...]
    cols[half:, :] = second[...]
    product = lax.dot_general(
        rows[...], cols[...], (((1,), (1,)), ((), ())), preferred_element_type=jnp.float32
    )
    mine_ref[...] = product[:ROWS]
    to_x = product[ROWS : 2 * ROWS].astype(jnp.bfloat16)
    c_ref[...] = product[2 * ROWS : 3 * ROWS].astype(jnp.bfloat16)
    to_xc = product[3 * ROWS :].astype(jnp.bfloat16)
    if len(refs) == 1:
        x_ref[:, :GROUP] = to_x
        x_ref[:, GROUP:] = to_xc
    else:
        x_ref[...] = to_x
        refs[0][...] = to_xc


def cross(rows, first, second, merged):
    narrow = jax.ShapeDtypeStruct((ROWS, GROUP), jnp.bfloat16)
    wide = jax.ShapeDtypeStruct((ROWS, 2 * GROUP), jnp.bfloat16)
    mine = jax.ShapeDtypeStruct((ROWS, GROUP), jnp.float32)
    return pl.pallas_call(
        cross_kernel,
        out_shape=[mine, narrow, wide] if merged else [mine, narrow, narrow, narrow],
        scratch_shapes=[pltpu.VMEM((4 * ROWS, DEPTH), jnp.bfloat16)],
        compiler_params=pltpu.CompilerParams(vmem_limit_bytes=12 << 20),
        cost_estimate=pl.CostEstimate(
            flops=2 * GROUP * GROUP * DEPTH, transcendentals=0, bytes_accessed=12 << 20
        ),
        name="cross",
    )(rows, first, second)


FIRST = 512


def first_cross_kernel(rows, pair0, pair1, mine_ref, c_ref, x_ref, here_ref, cols):
    cols[:ROWS, :] = pair0[ROWS:, :]
    cols[ROWS : 3 * ROWS, :] = pair1[...]
    cols[3 * ROWS :, :] = pair0[:ROWS, :]
    product = lax.dot_general(
        rows[...], cols[...], (((1,), (1,)), ((), ())), preferred_element_type=jnp.float32
    )
    mine_ref[...] = product[:ROWS]
    x_ref[:, :FIRST] = product[ROWS : 2 * ROWS, :FIRST].astype(jnp.bfloat16)
    c_ref[...] = product[2 * ROWS : 3 * ROWS].astype(jnp.bfloat16)
    x_ref[:, FIRST:] = product[3 * ROWS :, :FIRST].astype(jnp.bfloat16)
    here_ref[...] = lax.dot_general(
        rows[:ROWS, :], rows[...], (((1,), (1,)), ((), ())), preferred_element_type=jnp.float32
    )


def first_cross(rows, pair0, pair1):
    wide = jax.ShapeDtypeStruct((ROWS, GROUP), jnp.float32)
    return pl.pallas_call(
        first_cross_kernel,
        out_shape=[
            wide,
            jax.ShapeDtypeStruct((ROWS, GROUP), jnp.bfloat16),
            jax.ShapeDtypeStruct((ROWS, 2 * FIRST), jnp.bfloat16),
            wide,
        ],
        scratch_shapes=[pltpu.VMEM((4 * ROWS, DEPTH), jnp.bfloat16)],
        compiler_params=pltpu.CompilerParams(vmem_limit_bytes=12 << 20),
        cost_estimate=pl.CostEstimate(
            flops=2 * GROUP * GROUP * DEPTH, transcendentals=0, bytes_accessed=12 << 20
        ),
        name="cross",
    )(rows, pair0, pair1)


NEAR = (0, 1, -1, 2)
GROUPS = (
    ((1, 0), (-1, 0), (2, 0), (0, 0)),
    ((0, 1), (1, 1), (-1, -1), (2, -1)),
    ((-1, 1), (2, 1), (0, -1), (1, -1)),
    ((0, 2), (1, 2), (-1, 2), (2, 2)),
)
SPOT = {offset: (g, i) for g, group in enumerate(GROUPS) for i, offset in enumerate(group)}


def place_kernel(blocks, kinds, *refs):
    out, buf, sems = refs[-3:]
    pieces = {}
    for index, kind in enumerate(kinds):
        pieces[kind] = refs[index]
    chan = lax.axis_index("chan")
    z, y, spot, core = chan // 16, (chan // 4) % 4, chan % 4, chan % 2

    def copy(n):
        du, dv = blocks[n]
        dz, dy = jnp.where(core == 0, du, dv), jnp.where(core == 0, dv, du)
        unit_id = ((z + dz + 4) % 4) * 4 + (y + dy + 4) % 4
        start = pl.multiple_of(unit_id * GROUP, 128)
        return pltpu.make_async_copy(buf.at[n], out.at[:, pl.ds(start, GROUP)], sems.at[n])

    for slot in range(4):

        @pl.when(spot == slot)
        def _():
            for n, (du, dv) in enumerate(blocks):
                for turn in range(4):
                    g, i = SPOT[(dv, du) if turn % 2 else (du, dv)]
                    if (du, dv) == (0, 0):
                        ref, base, i = pieces[4, 0], 0, (0, 2, 1, 3)[turn]
                    else:
                        ref = pieces[turn, g]
                        split = turn == 3 and ref.shape[1] > GROUP
                        base = ref.shape[1] // 2 if split else 0
                    value = ref[:, base + i * ROWS : base + (i + 1) * ROWS].astype(jnp.float32)
                    at = (slot ^ turn) * ROWS
                    buf[n, :, at : at + ROWS] = value
                copy(n).start()

    for n in range(len(blocks)):
        copy(n).wait()


def place(blocks, pieces, out):
    vmem = pl.BlockSpec(memory_space=pltpu.VMEM)
    used = {(4, 0)} if (0, 0) in blocks else set()
    for du, dv in blocks:
        if (du, dv) != (0, 0):
            for turn in range(4):
                used.add((turn, SPOT[(dv, du) if turn % 2 else (du, dv)][0]))
    kinds = sorted(used, key=lambda kind: (kind[1], kind[0]))
    prior = () if out is None else (out,)
    return pl.pallas_call(
        lambda *refs: place_kernel(blocks, kinds, *refs),
        in_specs=[vmem] * len(kinds) + [pl.BlockSpec(memory_space=pl.ANY)] * len(prior),
        out_specs=pl.BlockSpec(memory_space=pl.ANY),
        out_shape=jax.ShapeDtypeStruct((ROWS, 16 * GROUP), jnp.float32),
        scratch_shapes=[
            pltpu.VMEM((len(blocks), ROWS, GROUP), jnp.float32),
            pltpu.SemaphoreType.DMA((len(blocks),)),
        ],
        input_output_aliases={len(kinds): 0} if prior else {},
        compiler_params=pltpu.CompilerParams(vmem_limit_bytes=16 << 20),
        name="place",
    )(*[pieces[kind] for kind in kinds], *prior)


def unit(index):
    return index // 16, index // 4 % 4, index // 2 % 2, index % 2


def join(z, y, x, c):
    return (z % 4) * 16 + (y % 4) * 4 + x * 2 + c


def from_first(shift):
    pairs = []
    for dst in range(64):
        z, y, x, c = unit(dst)
        src = join(z + shift, y, x, c) if c == 0 else join(z, y + shift, x, c)
        pairs.append((src, dst))
    return pairs


def from_second(shift):
    pairs = []
    for dst in range(64):
        z, y, x, c = unit(dst)
        src = join(z, y + shift, x, c) if c == 0 else join(z + shift, y, x, c)
        pairs.append((src, dst))
    return pairs


def flip(bits):
    return [(i, i ^ bits) for i in range(64)]


def local(traces, band_start, half_width):
    flat = jnp.transpose(traces, (1, 0, 2)).reshape(WINS * ROWS, SAMPLES)
    keep, send = whiten(flat, jnp.concatenate([band_start, half_width]))
    got = lax.ppermute(send, "band", [(0, 1), (1, 0)])
    own = normalize(keep, got)
    hold = lax.optimization_barrier

    def move(value, pairs):
        return lax.ppermute(value, "chan", pairs)

    over, ahead = move(own, flip(2)), move(own, from_first(1))
    behind, far = move(own, from_first(-1)), move(own, from_first(2))
    over, ahead, behind, far = hold((over, ahead, behind, far))
    mates = stack(own, over)
    across = move(mates, flip(1))
    pair0, pair1 = stack(own, ahead), stack(behind, far)
    up0, down1 = move(pair0, from_second(1)), move(pair1, from_second(-1))
    up1, down0 = move(pair1, from_second(1)), move(pair0, from_second(-1))
    rows = stack(mates, across)
    mine0, c0, x0, here = first_cross(rows, pair0, pair1)
    x0 = move(x0, flip(2))
    c0 = move(c0, flip(1))
    mine1, c1, x1 = cross(rows, up0, down1, True)
    x1, x0, c0, up0, down1 = hold((x1, x0, c0, up0, down1))
    up2, down2 = move(up0, from_second(1)), move(down1, from_second(-1))
    x1 = move(x1, flip(2))
    xc0 = move(x0, flip(1))
    c1 = move(c1, flip(1))
    mine2, c2, x2 = cross(rows, up1, down0, True)
    x2, c1, xc0 = hold((x2, c1, xc0))
    x2 = move(x2, flip(2))
    xc1 = move(x1, flip(1))
    c2 = move(c2, flip(1))
    mine3, c3, x3, xc3 = cross(rows, up2, down2, False)
    x3, xc3, x2, c2, xc1 = hold((x3, xc3, x2, c2, xc1))
    x3, xc3, c3 = move(x3, flip(2)), move(xc3, flip(3)), move(c3, flip(1))
    xc2 = move(x2, flip(1))
    early = [(du, dv) for du in NEAR for dv in NEAR if du != 2 and dv != 2]
    middle = [(0, 2), (1, 2), (-1, 2)]
    late = [(2, dv) for dv in NEAR]
    pieces = {(4, 0): here}
    for g, parts in enumerate(((mine0, c0, x0, xc0), (mine1, c1, x1, xc1), (mine2, c2, x2, xc2))):
        for turn in range(4):
            pieces[turn, g] = parts[turn]
    out = place(early, pieces, None)
    pieces[0, 3], pieces[2, 3] = mine3, x3
    out = place(middle, pieces, out)
    pieces[1, 3], pieces[3, 3] = c3, xc3
    return place(late, pieces, out)[None]


def solution(mesh):
    placed = (P("chan", "band", None), P(), P())
    return jax.shard_map(
        local, mesh=mesh, in_specs=placed, out_specs=P("band", "chan", None), check_vma=False
    )
```

```python
import math

import jax
import jax.numpy as jnp
from jax import lax
from jax.experimental import pallas as pl
from jax.experimental.pallas import tpu as pltpu
from jax.sharding import PartitionSpec as P

SAMPLES = 4096
BINS = 64
WINS = 6
ROWS = 160
DEPTH = 1536
GROUP = 640
STEP_ROWS = 320
CHUNK = 1024
LOAD = 2
PARTS = 128
TURN = 2.0 * math.pi / SAMPLES


def whiten_kernel(bands, x_hbm, keep_ref, send_ref, held, table, total, sems):
    def fetch(piece):
        block = pl.ds(piece * ROWS, ROWS)
        return pltpu.make_async_copy(x_hbm.at[block], held.at[block], sems.at[piece])

    for piece in range(0, WINS):
        fetch(piece).start()
    lane = lax.broadcasted_iota(jnp.int32, (1, 128), 1)
    freq = jnp.where(lane < BINS, bands[0] + lane, bands[1] + lane - BINS)
    coarse = lax.broadcasted_iota(jnp.int32, (SAMPLES // PARTS, 128), 0) * PARTS
    fine = lax.broadcasted_iota(jnp.int32, (PARTS, 128), 0)
    angle_a = ((freq * coarse) & (SAMPLES - 1)).astype(jnp.float32) * TURN
    angle_b = ((freq * fine) & (SAMPLES - 1)).astype(jnp.float32) * TURN
    root = 1.0 / math.sqrt(SAMPLES)
    cos_a, sin_a = jnp.cos(angle_a) * root, jnp.sin(angle_a) * root
    cos_b, sin_b = jnp.cos(angle_b), jnp.sin(angle_b)
    row = lax.broadcasted_iota(jnp.int32, (256, 128), 0) & 127
    col = lax.broadcasted_iota(jnp.int32, (256, 128), 1)
    half = jnp.where(col < BINS, bands[2], bands[3])
    inside = ((row < BINS) == (col < BINS)) & (jnp.abs(row - col) <= half)
    mask = inside.astype(jnp.float32).astype(jnp.bfloat16)
    bin_id = lane & (BINS - 1)
    width = jnp.where(lane < BINS, bands[2], bands[3])
    count = jnp.minimum(bin_id + width, BINS - 1) - jnp.maximum(bin_id - width, 0) + 1
    share = 1.0 / count.astype(jnp.float32)
    first = lax.broadcasted_iota(jnp.int32, (STEP_ROWS, 128), 1) < BINS
    mine = lax.axis_index("band") == 0

    for part in range(SAMPLES // PARTS):
        at = slice(part * PARTS, (part + 1) * PARTS)
        ca, sa = cos_a[part : part + 1], sin_a[part : part + 1]
        table[at, 0:128] = (ca * cos_b - sa * sin_b).astype(jnp.bfloat16)
        table[at, 128:256] = (-(sa * cos_b + ca * sin_b)).astype(jnp.bfloat16)

    for piece in range(0, WINS, LOAD):
        for i in range(LOAD):
            fetch(piece + i).wait()
        block = slice(piece * ROWS, (piece + LOAD) * ROWS)
        for at in range(0, SAMPLES, CHUNK):
            product = jnp.dot(
                held[block, at : at + CHUNK],
                table[at : at + CHUNK, :],
                preferred_element_type=jnp.float32,
            )
            if at == 0:
                total[block, :] = product
            else:
                total[block, :] += product

    for at in range(0, WINS * ROWS, STEP_ROWS):
        block = slice(at, at + STEP_ROWS)
        re, im = total[block, :128], total[block, 128:]
        amplitude = jnp.sqrt(re * re + im * im)
        high = amplitude.astype(jnp.bfloat16)
        low = (amplitude - high.astype(jnp.float32)).astype(jnp.bfloat16)
        sums = jnp.dot(
            jnp.concatenate([high, low], axis=1), mask, preferred_element_type=jnp.float32
        )
        gain = 1.0 / (sums * share + 1e-05)
        re, im = re * gain, im * gain
        turned = pltpu.roll(im, BINS, 1)
        band0 = jnp.where(first, re, turned)
        band1 = jnp.where(first, turned, re)
        keep_ref[block, :] = jnp.where(mine, band0, band1).astype(jnp.bfloat16)
        send_ref[block, :] = jnp.where(mine, band1, band0).astype(jnp.bfloat16)


def whiten(flat, bands):
    total = flat.shape[0]
    out = jax.ShapeDtypeStruct((total, 128), jnp.bfloat16)
    return pl.pallas_call(
        whiten_kernel,
        in_specs=[
            pl.BlockSpec(memory_space=pltpu.SMEM),
            pl.BlockSpec(memory_space=pltpu.HBM),
        ],
        out_shape=[out, out],
        scratch_shapes=[
            pltpu.VMEM((total, SAMPLES), jnp.bfloat16),
            pltpu.VMEM((SAMPLES, 256), jnp.bfloat16),
            pltpu.VMEM((total, 256), jnp.float32),
            pltpu.SemaphoreType.DMA((WINS,)),
        ],
        compiler_params=pltpu.CompilerParams(vmem_limit_bytes=53 << 20),
        name="whiten",
    )(bands, flat)


def normalize_kernel(keep_ref, got_ref, out_ref):
    energy = jnp.zeros((ROWS, 128), jnp.float32)
    for ref in (keep_ref, got_ref):
        for win in range(WINS):
            value = ref[win * ROWS : (win + 1) * ROWS, :].astype(jnp.float32)
            energy = energy + value * value
    scale = 1.0 / jnp.sqrt(jnp.sum(energy, axis=1, keepdims=True) + 1e-06)
    for side, ref in enumerate((keep_ref, got_ref)):
        for win in range(WINS):
            value = ref[win * ROWS : (win + 1) * ROWS, :].astype(jnp.float32)
            at = (side * WINS + win) * 128
            out_ref[:, at : at + 128] = (value * scale).astype(jnp.bfloat16)


def normalize(keep, got):
    return pl.pallas_call(
        normalize_kernel,
        out_shape=jax.ShapeDtypeStruct((ROWS, DEPTH), jnp.bfloat16),
        compiler_params=pltpu.CompilerParams(vmem_limit_bytes=8 << 20),
        name="normalize",
    )(keep, got)


def stack_kernel(*refs):
    at = 0
    for ref in refs[:-1]:
        refs[-1][at : at + ref.shape[0], :] = ref[...]
        at += ref.shape[0]


def stack(*shards):
    total = sum(shard.shape[0] for shard in shards)
    return pl.pallas_call(
        stack_kernel,
        out_shape=jax.ShapeDtypeStruct((total, DEPTH), jnp.bfloat16),
        compiler_params=pltpu.CompilerParams(vmem_limit_bytes=8 << 20),
        name="stack",
    )(*shards)


def cross_kernel(rows, first, second, mine_ref, c_ref, x_ref, *refs):
    cols = refs[-1]
    half = GROUP // 2
    cols[:half, :] = first[...]
    cols[half:, :] = second[...]
    product = lax.dot_general(
        rows[...], cols[...], (((1,), (1,)), ((), ())), preferred_element_type=jnp.float32
    )
    mine_ref[...] = product[:ROWS]
    to_x = product[ROWS : 2 * ROWS].astype(jnp.bfloat16)
    c_ref[...] = product[2 * ROWS : 3 * ROWS].astype(jnp.bfloat16)
    to_xc = product[3 * ROWS :].astype(jnp.bfloat16)
    if len(refs) == 1:
        x_ref[:, :GROUP] = to_x
        x_ref[:, GROUP:] = to_xc
    else:
        x_ref[...] = to_x
        refs[0][...] = to_xc


def cross(rows, first, second, merged):
    narrow = jax.ShapeDtypeStruct((ROWS, GROUP), jnp.bfloat16)
    wide = jax.ShapeDtypeStruct((ROWS, 2 * GROUP), jnp.bfloat16)
    mine = jax.ShapeDtypeStruct((ROWS, GROUP), jnp.float32)
    return pl.pallas_call(
        cross_kernel,
        out_shape=[mine, narrow, wide] if merged else [mine, narrow, narrow, narrow],
        scratch_shapes=[pltpu.VMEM((4 * ROWS, DEPTH), jnp.bfloat16)],
        compiler_params=pltpu.CompilerParams(vmem_limit_bytes=12 << 20),
        cost_estimate=pl.CostEstimate(
            flops=2 * GROUP * GROUP * DEPTH, transcendentals=0, bytes_accessed=12 << 20
        ),
        name="cross",
    )(rows, first, second)


FIRST = 512


def first_cross_kernel(rows, pair0, pair1, mine_ref, c_ref, x_ref, here_ref, cols):
    cols[:ROWS, :] = pair0[ROWS:, :]
    cols[ROWS : 3 * ROWS, :] = pair1[...]
    cols[3 * ROWS :, :] = pair0[:ROWS, :]
    product = lax.dot_general(
        rows[...], cols[...], (((1,), (1,)), ((), ())), preferred_element_type=jnp.float32
    )
    mine_ref[...] = product[:ROWS]
    x_ref[:, :FIRST] = product[ROWS : 2 * ROWS, :FIRST].astype(jnp.bfloat16)
    c_ref[...] = product[2 * ROWS : 3 * ROWS].astype(jnp.bfloat16)
    x_ref[:, FIRST:] = product[3 * ROWS :, :FIRST].astype(jnp.bfloat16)
    here_ref[...] = lax.dot_general(
        rows[:ROWS, :], rows[...], (((1,), (1,)), ((), ())), preferred_element_type=jnp.float32
    )


def first_cross(rows, pair0, pair1):
    wide = jax.ShapeDtypeStruct((ROWS, GROUP), jnp.float32)
    return pl.pallas_call(
        first_cross_kernel,
        out_shape=[
            wide,
            jax.ShapeDtypeStruct((ROWS, GROUP), jnp.bfloat16),
            jax.ShapeDtypeStruct((ROWS, 2 * FIRST), jnp.bfloat16),
            wide,
        ],
        scratch_shapes=[pltpu.VMEM((4 * ROWS, DEPTH), jnp.bfloat16)],
        compiler_params=pltpu.CompilerParams(vmem_limit_bytes=12 << 20),
        cost_estimate=pl.CostEstimate(
            flops=2 * GROUP * GROUP * DEPTH, transcendentals=0, bytes_accessed=12 << 20
        ),
        name="cross",
    )(rows, pair0, pair1)


NEAR = (0, 1, -1, 2)
GROUPS = (
    ((1, 0), (-1, 0), (2, 0), (0, 0)),
    ((0, 1), (1, 1), (-1, -1), (2, -1)),
    ((-1, 1), (2, 1), (0, -1), (1, -1)),
    ((0, 2), (1, 2), (-1, 2), (2, 2)),
)
SPOT = {offset: (g, i) for g, group in enumerate(GROUPS) for i, offset in enumerate(group)}


def place_kernel(blocks, kinds, *refs):
    out, buf, sems = refs[-3:]
    pieces = {}
    for index, kind in enumerate(kinds):
        pieces[kind] = refs[index]
    chan = lax.axis_index("chan")
    z, y, spot, core = chan // 16, (chan // 4) % 4, chan % 4, chan % 2

    def copy(n):
        du, dv = blocks[n]
        dz, dy = jnp.where(core == 0, du, dv), jnp.where(core == 0, dv, du)
        unit_id = ((z + dz + 4) % 4) * 4 + (y + dy + 4) % 4
        start = pl.multiple_of(unit_id * GROUP, 128)
        return pltpu.make_async_copy(buf.at[n], out.at[:, pl.ds(start, GROUP)], sems.at[n])

    for slot in range(4):

        @pl.when(spot == slot)
        def _():
            for n, (du, dv) in enumerate(blocks):
                for turn in range(4):
                    g, i = SPOT[(dv, du) if turn % 2 else (du, dv)]
                    if (du, dv) == (0, 0):
                        ref, base, i = pieces[4, 0], 0, (0, 2, 1, 3)[turn]
                    else:
                        ref = pieces[turn, g]
                        split = turn == 3 and ref.shape[1] > GROUP
                        base = ref.shape[1] // 2 if split else 0
                    value = ref[:, base + i * ROWS : base + (i + 1) * ROWS].astype(jnp.float32)
                    at = (slot ^ turn) * ROWS
                    buf[n, :, at : at + ROWS] = value
                copy(n).start()

    for n in range(len(blocks)):
        copy(n).wait()


def place(blocks, pieces, out):
    vmem = pl.BlockSpec(memory_space=pltpu.VMEM)
    used = {(4, 0)} if (0, 0) in blocks else set()
    for du, dv in blocks:
        if (du, dv) != (0, 0):
            for turn in range(4):
                used.add((turn, SPOT[(dv, du) if turn % 2 else (du, dv)][0]))
    kinds = sorted(used, key=lambda kind: (kind[1], kind[0]))
    prior = () if out is None else (out,)
    return pl.pallas_call(
        lambda *refs: place_kernel(blocks, kinds, *refs),
        in_specs=[vmem] * len(kinds) + [pl.BlockSpec(memory_space=pl.ANY)] * len(prior),
        out_specs=pl.BlockSpec(memory_space=pl.ANY),
        out_shape=jax.ShapeDtypeStruct((ROWS, 16 * GROUP), jnp.float32),
        scratch_shapes=[
            pltpu.VMEM((len(blocks), ROWS, GROUP), jnp.float32),
            pltpu.SemaphoreType.DMA((len(blocks),)),
        ],
        input_output_aliases={len(kinds): 0} if prior else {},
        compiler_params=pltpu.CompilerParams(vmem_limit_bytes=16 << 20),
        name="place",
    )(*[pieces[kind] for kind in kinds], *prior)


def unit(index):
    return index // 16, index // 4 % 4, index // 2 % 2, index % 2


def join(z, y, x, c):
    return (z % 4) * 16 + (y % 4) * 4 + x * 2 + c


def from_first(shift):
    pairs = []
    for dst in range(64):
        z, y, x, c = unit(dst)
        src = join(z + shift, y, x, c) if c == 0 else join(z, y + shift, x, c)
        pairs.append((src, dst))
    return pairs


def from_second(shift):
    pairs = []
    for dst in range(64):
        z, y, x, c = unit(dst)
        src = join(z, y + shift, x, c) if c == 0 else join(z + shift, y, x, c)
        pairs.append((src, dst))
    return pairs


def flip(bits):
    return [(i, i ^ bits) for i in range(64)]


def local(traces, band_start, half_width):
    flat = jnp.transpose(traces, (1, 0, 2)).reshape(WINS * ROWS, SAMPLES)
    keep, send = whiten(flat, jnp.concatenate([band_start, half_width]))
    got = lax.ppermute(send, "band", [(0, 1), (1, 0)])
    own = normalize(keep, got)
    hold = lax.optimization_barrier

    def move(value, pairs):
        return lax.ppermute(value, "chan", pairs)

    ahead, over = move(own, from_first(1)), move(own, flip(2))
    behind, far = move(own, from_first(-1)), move(own, from_first(2))
    ahead, over, behind, far = hold((ahead, over, behind, far))
    mates = stack(own, over)
    across = move(mates, flip(1))
    pair0, pair1 = stack(own, ahead), stack(behind, far)
    up0, down1 = move(pair0, from_second(1)), move(pair1, from_second(-1))
    up1, down0 = move(pair1, from_second(1)), move(pair0, from_second(-1))
    rows = stack(mates, across)
    mine0, c0, x0, here = first_cross(rows, pair0, pair1)
    x0 = move(x0, flip(2))
    c0 = move(c0, flip(1))
    mine1, c1, x1 = cross(rows, up0, down1, True)
    x1, x0, c0, up0, down1 = hold((x1, x0, c0, up0, down1))
    up2, down2 = move(up0, from_second(1)), move(down1, from_second(-1))
    x1 = move(x1, flip(2))
    xc0 = move(x0, flip(1))
    c1 = move(c1, flip(1))
    mine2, c2, x2 = cross(rows, up1, down0, True)
    x2, c1, xc0 = hold((x2, c1, xc0))
    x2 = move(x2, flip(2))
    xc1 = move(x1, flip(1))
    c2 = move(c2, flip(1))
    mine3, c3, x3, xc3 = cross(rows, up2, down2, False)
    x3, xc3, x2, c2, xc1 = hold((x3, xc3, x2, c2, xc1))
    x3, xc3, c3 = move(x3, flip(2)), move(xc3, flip(3)), move(c3, flip(1))
    xc2 = move(x2, flip(1))
    early = [(du, dv) for du in NEAR for dv in NEAR if du != 2 and dv != 2]
    middle = [(0, 2), (1, 2), (-1, 2)]
    late = [(2, dv) for dv in NEAR]
    pieces = {(4, 0): here}
    for g, parts in enumerate(((mine0, c0, x0, xc0), (mine1, c1, x1, xc1), (mine2, c2, x2, xc2))):
        for turn in range(4):
            pieces[turn, g] = parts[turn]
    out = place(early, pieces, None)
    pieces[0, 3], pieces[2, 3] = mine3, x3
    out = place(middle, pieces, out)
    pieces[1, 3], pieces[3, 3] = c3, xc3
    return place(late, pieces, out)[None]


def solution(mesh):
    placed = (P("chan", "band", None), P(), P())
    return jax.shard_map(
        local, mesh=mesh, in_specs=placed, out_specs=P("band", "chan", None), check_vma=False
    )
```
